32 devices in a mesh: gz: 16 (over z, x, core), gy: 2 (over y).
Axes of the slice: x: 2, y: 2, z: 4, core: 2. Of those that a mesh axis runs over, the one named last changes fastest.
Arguments:
- vorticity: float32 [256, 128, 512], P('gz', 'gy'), may hold values from -12 to 12
- keep_one: int32 [7, 128, 64, 256], P(None, 'gz', 'gy'), may hold values 0 or 1
- keep_two: int32 [7, 64, 32, 128], P(None, 'gz', 'gy'), may hold values 0 or 1
- keep_three: int32 [7, 32, 16, 64], P(None, 'gz', 'gy'), may hold values 0 or 1
- keep_four: int32 [7, 16, 8, 32], P(None, 'gz', 'gy'), may hold values 0 or 1
- keep_coarse: int32 [16, 8, 32], P('gz', 'gy'), may hold values 0 or 1
Outputs:
- coherent: float32 [256, 128, 512], P('gz', 'gy')
The draws below stay inside these ranges and needn't reach their ends.
All inputs are finite; a program needn't handle non-finite values. No bound on the sum of `keep_one` or of `keep_two` or of `keep_three` or of `keep_four` or of `keep_coarse` on one device may be relied on, other than what follows from the above.
Results may differ from the reference program's by a relative error of at most 0.00017.
Values sent between devices are 32-bit elements; how exact they have to be, the bound alone decides.
A program may use at most 128 MiB of HBM per device.

```python
import math
import jax
import jax.numpy as jnp
from jax import lax

NX = 512
NZ = 256
NY = 128


def draw_vorticity(key, part):
    rough_key = jax.random.fold_in(key, 11)
    z_key = jax.random.fold_in(key, 12)
    y_key = jax.random.fold_in(key, 13)
    x_key = jax.random.fold_in(key, 14)
    phase_key = jax.random.fold_in(key, 15)
    waves_z = jax.random.randint(z_key, (6,), 1, 22).astype(jnp.float32)
    waves_y = jax.random.randint(y_key, (6,), 1, 22).astype(jnp.float32)
    waves_x = jax.random.randint(x_key, (6,), 0, max(2, NX // 24)).astype(jnp.float32)
    phases = jax.random.uniform(phase_key, (6,), jnp.float32, 0.0, 2.0 * math.pi)
    z_pos = jnp.arange(NZ, dtype=jnp.float32)[:, None, None] / NZ
    y_pos = jnp.arange(NY, dtype=jnp.float32)[None, :, None] / NY
    x_pos = jnp.arange(NX, dtype=jnp.float32)[None, None, :] / NX
    smooth = jnp.zeros((NZ, NY, NX), jnp.float32)
    for mode_no in range(6):
        argument = 2.0 * math.pi * (waves_z[mode_no] * z_pos + waves_y[mode_no] * y_pos + waves_x[mode_no] * x_pos)
        smooth = smooth + jnp.sin(argument + phases[mode_no])
    rough = jnp.clip(jax.random.normal(rough_key, (NZ, NY, NX), jnp.float32), -6.0, 6.0)
    return rough + 0.8 * smooth


def with_ends(array, rng, least, largest):
    shape = array.shape
    index_at = [jax.random.randint(jax.random.fold_in(rng, axis), (), 0, shape[axis]) for axis in range(len(shape))]
    array = array.at[tuple(index_at)].set(least)
    longest = shape.index(max(shape))
    index_at[longest] = (index_at[longest] + 1) % shape[longest]
    return array.at[tuple(index_at)].set(largest)


def setup_inputs(seed: int = 0) -> dict:
    key_of = jax.random.split(jax.random.key(seed), 7)
    return {
        "vorticity": draw_vorticity(jax.random.fold_in(key_of[6], 71), 0),
        "keep_one": with_ends((jax.random.randint(key_of[1], (7, NZ // 2, NY // 2, NX // 2), 0, 2) < 1).astype(jnp.int32), jax.random.fold_in(key_of[1], 1), 0, 1),
        "keep_two": with_ends((jax.random.randint(key_of[2], (7, NZ // 4, NY // 4, NX // 4), 0, 2) < 1).astype(jnp.int32), jax.random.fold_in(key_of[2], 1), 0, 1),
        "keep_three": with_ends((jax.random.randint(key_of[3], (7, NZ // 8, NY // 8, NX // 8), 0, 2) < 1).astype(jnp.int32), jax.random.fold_in(key_of[3], 1), 0, 1),
        "keep_four": with_ends((jax.random.randint(key_of[4], (7, NZ // 16, NY // 16, NX // 16), 0, 2) < 1).astype(jnp.int32), jax.random.fold_in(key_of[4], 1), 0, 1),
        "keep_coarse": with_ends((jax.random.randint(key_of[5], (NZ // 16, NY // 16, NX // 16), 0, 2) < 1).astype(jnp.int32), jax.random.fold_in(key_of[5], 1), 0, 1),
    }


low_taps = (0.11154074335008017, 0.4946238903983854, 0.7511339080215775, 0.3152503517092432,
            -0.22626469396516913, -0.12976686756709563, 0.09750160558707936, 0.02752286553001629,
            -0.031582039318031156, 0.0005538422009938016, 0.004777257511010651, -0.00107730108499558)
high_taps = tuple(((-1.0) ** k) * low_taps[11 - k] for k in range(12))


def wrap_right(source, axis_dim, rim_width):
    length = source.shape[axis_dim]
    copies = 1 + (rim_width + length - 1) // length
    repeated = jnp.concatenate([source] * copies, axis=axis_dim)
    return lax.slice_in_dim(repeated, 0, length + rim_width, axis=axis_dim)


def wrap_left(source, axis_dim, rim_width):
    length = source.shape[axis_dim]
    copies = 1 + (rim_width + length - 1) // length
    repeated = jnp.concatenate([source] * copies, axis=axis_dim)
    total_len = copies * length
    return lax.slice_in_dim(repeated, total_len - length - rim_width, total_len, axis=axis_dim)


def split_pair(extended, axis_dim, length):
    low_part = None
    high_part = None
    for k in range(12):
        sliced = lax.slice_in_dim(extended, k, k + length - 1, stride=2, axis=axis_dim)
        if k == 0:
            low_part = low_taps[k] * sliced
            high_part = high_taps[k] * sliced
        else:
            low_part = low_part + low_taps[k] * sliced
            high_part = high_part + high_taps[k] * sliced
    return low_part, high_part


def merge_pair(low_ext, high_ext, axis_dim, coarse_len):
    even_part = None
    odd_part = None
    for t in range(6):
        low_slice = lax.slice_in_dim(low_ext, 5 - t, 5 - t + coarse_len, axis=axis_dim)
        high_slice = lax.slice_in_dim(high_ext, 5 - t, 5 - t + coarse_len, axis=axis_dim)
        even_term = low_taps[2 * t] * low_slice + high_taps[2 * t] * high_slice
        odd_term = low_taps[2 * t + 1] * low_slice + high_taps[2 * t + 1] * high_slice
        if t == 0:
            even_part = even_term
            odd_part = odd_term
        else:
            even_part = even_part + even_term
            odd_part = odd_part + odd_term
    paired = jnp.stack([even_part, odd_part], axis=axis_dim + 1)
    new_shape = even_part.shape[:axis_dim] + (2 * coarse_len,) + even_part.shape[axis_dim + 1:]
    return paired.reshape(new_shape)


def analyse(source, axis_dim):
    return split_pair(wrap_right(source, axis_dim, 10), axis_dim, source.shape[axis_dim])


def synthesize(low_part, high_part, axis_dim):
    coarse_len = low_part.shape[axis_dim]
    return merge_pair(wrap_left(low_part, axis_dim, 5), wrap_left(high_part, axis_dim, 5), axis_dim, coarse_len)


def reference(vorticity, keep_one, keep_two, keep_three, keep_four, keep_coarse):
    keep_list = (keep_one, keep_two, keep_three, keep_four)
    approx = vorticity
    kept_list = []
    for level_no in range(4):
        subbands = list(analyse(approx, 2))
        for axis_dim in (1, 0):
            pair_list = [analyse(member, axis_dim) for member in subbands]
            subbands = [p[0] for p in pair_list] + [p[1] for p in pair_list]
        kept_list.append(jnp.stack(subbands[1:]) * keep_list[level_no].astype(jnp.float32))
        approx = subbands[0]
    rebuilt = approx * keep_coarse.astype(jnp.float32)
    for level_no in (3, 2, 1, 0):
        subbands = [rebuilt] + [kept_list[level_no][b] for b in range(7)]
        subbands = [synthesize(subbands[b], subbands[b + 4], 0) for b in range(4)]
        subbands = [synthesize(subbands[b], subbands[b + 2], 1) for b in range(2)]
        rebuilt = synthesize(subbands[0], subbands[1], 2)
    return rebuilt
```

```python
import functools

import jax
import jax.numpy as jnp
import ml_dtypes
import numpy as np
from jax import lax
from jax.experimental import pallas as pl
from jax.experimental.pallas import tpu as pltpu
from jax.sharding import PartitionSpec as P

low_taps = (
    0.11154074335008017,
    0.4946238903983854,
    0.7511339080215775,
    0.3152503517092432,
    -0.22626469396516913,
    -0.12976686756709563,
    0.09750160558707936,
    0.02752286553001629,
    -0.031582039318031156,
    0.0005538422009938016,
    0.004777257511010651,
    -0.00107730108499558,
)
high_taps = tuple(((-1.0) ** k * low_taps[11 - k] for k in range(12)))
LEVELS = 4
MESH = pl.DeviceIdType.MESH
BF16 = jnp.bfloat16
F32 = jnp.float32


def halves(matrix):
    matrix = matrix.astype(np.float32)
    high = matrix.astype(ml_dtypes.bfloat16)
    low = (matrix - high.astype(np.float32)).astype(ml_dtypes.bfloat16)
    return np.stack([high, low])


def x_matrix(x_len):
    half = x_len // 2
    matrix = np.zeros((x_len, x_len))
    for i in range(half):
        for k in range(12):
            matrix[(2 * i + k) % x_len, i] += low_taps[k]
            matrix[(2 * i + k) % x_len, half + i] += high_taps[k]
    return matrix


def y_split_matrix(y_len, ext_len):
    half = y_len // 2
    matrix = np.zeros((y_len, ext_len))
    for i in range(half):
        for k in range(12):
            matrix[i, 2 * i + k] = low_taps[k]
            matrix[half + i, 2 * i + k] = high_taps[k]
    return matrix


def y_merge_matrix(coarse, ext_len):
    first = ext_len - coarse
    matrix = np.zeros((2 * coarse, 2 * ext_len))
    for j in range(2 * coarse):
        for t in range(6):
            k = 2 * t + j % 2
            c = j // 2 - t + first
            matrix[j, c] = low_taps[k]
            matrix[j, ext_len + c] = high_taps[k]
    return matrix


class Level:
    def __init__(self, z, y, x):
        self.z, self.y, self.x = z, y, x
        self.zc, self.yc, self.xc = z // 2, y // 2, x // 2
        self.rim_rows = min(y, 16)
        self.rim_hops = 16 // self.rim_rows
        self.y_ext = y + 16
        self.z_ext = z + 10
        self.block = min(self.yc, 8)
        self.back_hops = 8 // self.block
        self.blocks = self.yc // self.block + self.back_hops
        self.yc_ext = self.blocks * self.block
        self.zc_ext = self.zc + 5


def hop_list(length, rim):
    pieces = [(0, 0, length)]
    done = 0
    hop = 1
    while done < rim:
        take = min(length, rim - done)
        pieces.append((hop, done, take))
        done += take
        hop += 1
    return pieces


def split_product(data, pair_ref):
    high = data.astype(BF16)
    low = (data - high.astype(F32)).astype(BF16)
    out = jnp.dot(high, pair_ref[0], preferred_element_type=F32)
    out += jnp.dot(low, pair_ref[0], preferred_element_type=F32)
    return out + jnp.dot(high, pair_ref[1], preferred_element_type=F32)


def product_split(pair_ref, data):
    high = data.astype(BF16)
    low = (data - high.astype(F32)).astype(BF16)
    out = jnp.dot(pair_ref[0], high, preferred_element_type=F32)
    out += jnp.dot(pair_ref[0], low, preferred_element_type=F32)
    return out + jnp.dot(pair_ref[1], high, preferred_element_type=F32)


def kernel(levels, nz, ny, count, *refs):
    field = refs[0]
    keeps = refs[1:5]
    coarse = refs[5]
    x_fwd = refs[6:10]
    x_inv = refs[10:14]
    y_fwd = refs[14:18]
    y_inv = refs[18:22]
    out = refs[22]
    exts = refs[23:27]
    zbufs = refs[27:31]
    coefs = refs[31:35]
    sbufs = refs[35:39]
    ybufs = refs[39:43]
    local_sem, send_sem, recv_sem = refs[43:46]
    gz = lax.axis_index("gz")
    gy = lax.axis_index("gy")

    def device(dz, dy):
        return (lax.rem(gz + (dz + nz) % nz, nz), lax.rem(gy + (dy + ny) % ny, ny))

    load = pltpu.make_async_copy(field, exts[0].at[0 : levels[0].z, 0 : levels[0].y], local_sem)
    load.start()
    offsets = sorted(
        {(dz % nz, dy % ny) for dz in range(-5, 6) for dy in range(-2, 3)} - {(0, 0)}
    )
    barrier = pltpu.get_barrier_semaphore()
    for dz, dy in offsets:
        pl.semaphore_signal(barrier, inc=1, device_id=device(dz, dy), device_id_type=MESH)
    pl.semaphore_wait(barrier, len(offsets))

    used = [0]
    sends = []

    def send(src, dst, dz, dy):
        at = used[0]
        used[0] += 1
        copy = pltpu.make_async_remote_copy(
            src_ref=src,
            dst_ref=dst,
            send_sem=send_sem.at[at],
            recv_sem=recv_sem.at[at],
            device_id=device(dz, dy),
            device_id_type=MESH,
        )
        copy.start()
        sends.append(copy)
        return copy

    def send_rim(lv, source, ext):
        copies = []
        for hz, z_at, z_take in hop_list(lv.z, 10):
            for hy in range(lv.rim_hops + 1):
                if hy and hy % ny == 0 or (hz == 0 and hy == 0):
                    continue
                rows = lv.y if hy == 0 else lv.rim_rows
                z_to = 0 if hz == 0 else lv.z + z_at
                y_to = 0 if hy == 0 else lv.y + (hy - 1) * lv.rim_rows
                copies.append(
                    send(
                        source.at[0:z_take, 0:rows],
                        ext.at[z_to : z_to + z_take, y_to : y_to + rows],
                        -hz,
                        -hy,
                    )
                )
        return copies

    def send_back(lv, coef, first, last):
        copies = []
        own = lv.back_hops
        for hz, z_at, z_take in hop_list(lv.zc, 5):
            for hy in range(lv.back_hops + 1):
                if hy and hy % ny == 0 or (hz == 0 and hy == 0):
                    continue
                z_from = 5 if hz == 0 else 5 + lv.zc - z_take
                z_to = 5 if hz == 0 else 5 - z_at - z_take
                y_from = own if hy == 0 else lv.blocks - 1
                y_take = lv.blocks - own if hy == 0 else 1
                y_to = own if hy == 0 else own - hy
                copies.append(
                    send(
                        coef.at[first:last, z_from : z_from + z_take, y_from : y_from + y_take],
                        coef.at[first:last, z_to : z_to + z_take, y_to : y_to + y_take],
                        hz,
                        hy,
                    )
                )
        return copies

    detail_copies = []
    for no, lv in enumerate(levels):
        ext, zbuf, coef, keep = exts[no], zbufs[no], coefs[no], keeps[no]
        copies = send_rim(lv, field if no == 0 else ext, ext)
        if no == 0:
            load.wait()
        for copy in copies:
            copy.wait_recv()
        for hy in range(1, lv.rim_hops + 1):
            if hy % ny == 0:
                y_to = lv.y + (hy - 1) * lv.rim_rows
                ext[:, y_to : y_to + lv.rim_rows, :] = ext[:, 0 : lv.rim_rows, :]
        chunk = 16 if lv.y_ext % 16 == 0 else 8
        steps = lv.y_ext // chunk

        def z_split(step, carry, lv=lv, ext=ext, zbuf=zbuf, chunk=chunk, steps=steps):
            i = step // steps
            row = pl.multiple_of((step % steps) * chunk, chunk)
            low = high = None
            for k in range(12):
                part = ext[2 * i + k, pl.ds(row, chunk), :]
                low = low_taps[k] * part if k == 0 else low + low_taps[k] * part
                high = high_taps[k] * part if k == 0 else high + high_taps[k] * part
            zbuf[i, pl.ds(row, chunk), :] = low
            zbuf[lv.zc + i, pl.ds(row, chunk), :] = high
            return carry

        lax.fori_loop(0, lv.zc * steps, z_split, 0)
        group = min(lv.z, 4)

        def x_split(step, carry, lv=lv, zbuf=zbuf, group=group, no=no):
            at = pl.ds(step * group, group)
            rows = zbuf[at].reshape(group * lv.y_ext, lv.x)
            zbuf[at] = split_product(rows, x_fwd[no]).reshape(group, lv.y_ext, lv.x)
            return carry

        lax.fori_loop(0, lv.z // group, x_split, 0)

        def y_split(i, carry, lv=lv, zbuf=zbuf, coef=coef, keep=keep, no=no):
            for bz in range(2):
                mixed = product_split(y_fwd[no], zbuf[bz * lv.zc + i])
                for by in range(2):
                    part = mixed[by * lv.yc : (by + 1) * lv.yc]
                    for bx in range(2):
                        band = 4 * bz + 2 * by + bx
                        piece = part[:, bx * lv.xc : (bx + 1) * lv.xc]
                        if band:
                            piece = piece * keep[band - 1, i].astype(F32)
                        elif no < LEVELS - 1:
                            exts[no + 1][i, 0 : lv.yc, :] = piece
                            continue
                        else:
                            piece = piece * coarse[i].astype(F32)
                        shaped = piece.reshape(lv.yc // lv.block, lv.block, lv.xc)
                        lanes = slice(bx * lv.xc, (bx + 1) * lv.xc)
                        coef[2 * bz + by, 5 + i, lv.back_hops : lv.blocks, :, lanes] = shaped
            return carry

        lax.fori_loop(0, lv.zc, y_split, 0)
        if no == LEVELS - 1:
            detail_copies.append([])
        else:
            detail_copies.append((lv, coef))

    early = [None] * LEVELS
    for no in range(LEVELS - 1, -1, -1):
        lv, coef, sbuf, ybuf = levels[no], coefs[no], sbufs[no], ybufs[no]
        late = send_back(lv, coef, 0, 1)
        if no == LEVELS - 1:
            for each in range(LEVELS - 1, -1, -1):
                early[each] = send_back(levels[each], coefs[each], 1, 4)
        for copy in late + early[no]:
            copy.wait_recv()
        for hy in range(1, lv.back_hops + 1):
            if hy % ny == 0:
                coef[:, :, lv.back_hops - hy] = coef[:, :, lv.blocks - 1]
        z_group = lv.zc_ext

        def x_merge(b, carry, lv=lv, coef=coef, sbuf=sbuf, no=no):
            if lv.block == 8:
                rows = coef[b].reshape(lv.zc_ext * lv.yc_ext, lv.x)
                sbuf[b] = split_product(rows, x_inv[no]).reshape(lv.zc_ext, lv.yc_ext, lv.x)
            else:
                for z in range(lv.zc_ext):
                    rows = jnp.concatenate([coef[b, z, j] for j in range(lv.blocks)], axis=0)
                    sbuf[b, z] = split_product(rows, x_inv[no])
            return carry

        lax.fori_loop(0, 4, x_merge, 0)

        def y_merge(z, carry, lv=lv, sbuf=sbuf, ybuf=ybuf, no=no):
            for bz in range(2):
                pair = jnp.concatenate([sbuf[2 * bz, z], sbuf[2 * bz + 1, z]], axis=0)
                ybuf[bz, z] = product_split(y_inv[no], pair)
            return carry

        lax.fori_loop(0, lv.zc_ext, y_merge, 0)
        chunk = min(lv.y, 16)
        if no:
            chunk = min(chunk, levels[no - 1].block)
        steps = lv.y // chunk

        def z_merge(step, carry, lv=lv, ybuf=ybuf, no=no, chunk=chunk, steps=steps):
            i = step // steps
            at = step % steps
            row = pl.multiple_of(at * chunk, chunk)
            even = odd = None
            for t in range(6):
                low = ybuf[0, i + 5 - t, pl.ds(row, chunk), :]
                high = ybuf[1, i + 5 - t, pl.ds(row, chunk), :]
                even_term = low_taps[2 * t] * low + high_taps[2 * t] * high
                odd_term = low_taps[2 * t + 1] * low + high_taps[2 * t + 1] * high
                even = even_term if t == 0 else even + even_term
                odd = odd_term if t == 0 else odd + odd_term
            for p, value in ((0, even), (1, odd)):
                if no == 0:
                    out[2 * i + p, pl.ds(row, chunk), :] = value
                else:
                    own = levels[no - 1].back_hops
                    coefs[no - 1][0, 5 + 2 * i + p, own + at, :, 0 : lv.x] = value
            return carry

        lax.fori_loop(0, lv.zc * steps, z_merge, 0)
    for copy in sends:
        copy.wait_send()
    assert used[0] == count


def solution(mesh):
    nz, ny = mesh.shape["gz"], mesh.shape["gy"]

    def on_device(field, k1, k2, k3, k4, coarse):
        z, y, x = field.shape
        levels = [Level(z >> n, y >> n, x >> n) for n in range(LEVELS)]
        count = 0
        for lv in levels:
            rim = len(hop_list(lv.z, 10)) * sum(h % ny != 0 or h == 0 for h in range(lv.rim_hops + 1))
            back = len(hop_list(lv.zc, 5)) * sum(h % ny != 0 or h == 0 for h in range(lv.back_hops + 1))
            count += rim - 1 + 2 * (back - 1)
        x_pairs = [halves(x_matrix(lv.x)) for lv in levels]
        xt_pairs = [halves(x_matrix(lv.x).T) for lv in levels]
        y_pairs = [halves(y_split_matrix(lv.y, lv.y_ext)) for lv in levels]
        yt_pairs = [halves(y_merge_matrix(lv.yc, lv.yc_ext)) for lv in levels]
        mats = [jnp.asarray(m) for m in x_pairs + xt_pairs + y_pairs + yt_pairs]
        vmem = pl.BlockSpec(memory_space=pltpu.VMEM)
        scratch = [pltpu.VMEM((lv.z_ext, lv.y_ext, lv.x), F32) for lv in levels]
        scratch += [pltpu.VMEM((lv.z, lv.y_ext, lv.x), F32) for lv in levels]
        scratch += [pltpu.VMEM((4, lv.zc_ext, lv.blocks, lv.block, lv.x), F32) for lv in levels]
        scratch += [pltpu.VMEM((4, lv.zc_ext, lv.yc_ext, lv.x), F32) for lv in levels]
        scratch += [pltpu.VMEM((2, lv.zc_ext, lv.y, lv.x), F32) for lv in levels]
        scratch += [
            pltpu.SemaphoreType.DMA,
            pltpu.SemaphoreType.DMA((count,)),
            pltpu.SemaphoreType.DMA((count,)),
        ]
        return pl.pallas_call(
            functools.partial(kernel, levels, nz, ny, count),
            out_shape=jax.ShapeDtypeStruct((z, y, x), F32),
            in_specs=[pl.BlockSpec(memory_space=pl.ANY)] + [vmem] * (5 + len(mats)),
            out_specs=vmem,
            scratch_shapes=scratch,
            compiler_params=pltpu.CompilerParams(
                collective_id=0, has_side_effects=True, vmem_limit_bytes=60 * 1024 * 1024
            ),
        )(field, k1, k2, k3, k4, coarse, *mats)

    in_specs = (
        P("gz", "gy", None),
        P(None, "gz", "gy", None),
        P(None, "gz", "gy", None),
        P(None, "gz", "gy", None),
        P(None, "gz", "gy", None),
        P("gz", "gy", None),
    )
    return jax.shard_map(
        on_device, mesh=mesh, in_specs=in_specs, out_specs=P("gz", "gy", None), check_vma=False
    )
```

```python
import functools

import jax
import jax.numpy as jnp
import ml_dtypes
import numpy as np
from jax import lax
from jax.experimental import pallas as pl
from jax.experimental.pallas import tpu as pltpu
from jax.sharding import PartitionSpec as P

low_taps = (
    0.11154074335008017,
    0.4946238903983854,
    0.7511339080215775,
    0.3152503517092432,
    -0.22626469396516913,
    -0.12976686756709563,
    0.09750160558707936,
    0.02752286553001629,
    -0.031582039318031156,
    0.0005538422009938016,
    0.004777257511010651,
    -0.00107730108499558,
)
high_taps = tuple(((-1.0) ** k * low_taps[11 - k] for k in range(12)))
LEVELS = 4
MESH = pl.DeviceIdType.MESH
BF16 = jnp.bfloat16
F32 = jnp.float32


def halves(matrix):
    matrix = matrix.astype(np.float32)
    high = matrix.astype(ml_dtypes.bfloat16)
    low = (matrix - high.astype(np.float32)).astype(ml_dtypes.bfloat16)
    return np.stack([high, low])


def x_matrix(x_len):
    half = x_len // 2
    matrix = np.zeros((x_len, x_len))
    for i in range(half):
        for k in range(12):
            matrix[(2 * i + k) % x_len, i] += low_taps[k]
            matrix[(2 * i + k) % x_len, half + i] += high_taps[k]
    return matrix


def y_split_matrix(y_len, ext_len):
    half = y_len // 2
    matrix = np.zeros((y_len, ext_len))
    for i in range(half):
        for k in range(12):
            matrix[i, 2 * i + k] = low_taps[k]
            matrix[half + i, 2 * i + k] = high_taps[k]
    return matrix


def y_merge_matrix(coarse, ext_len):
    first = ext_len - coarse
    matrix = np.zeros((2 * coarse, 2 * ext_len))
    for j in range(2 * coarse):
        for t in range(6):
            k = 2 * t + j % 2
            c = j // 2 - t + first
            matrix[j, c] = low_taps[k]
            matrix[j, ext_len + c] = high_taps[k]
    return matrix


class Level:
    def __init__(self, z, y, x):
        self.z, self.y, self.x = z, y, x
        self.zc, self.yc, self.xc = z // 2, y // 2, x // 2
        self.rim_rows = min(y, 16)
        self.rim_hops = 16 // self.rim_rows
        self.y_ext = y + 16
        self.z_ext = z + 10
        self.block = min(self.yc, 8)
        self.back_hops = 8 // self.block
        self.blocks = self.yc // self.block + self.back_hops
        self.yc_ext = self.blocks * self.block
        self.zc_ext = self.zc + 5


def hop_list(length, rim):
    pieces = [(0, 0, length)]
    done = 0
    hop = 1
    while done < rim:
        take = min(length, rim - done)
        pieces.append((hop, done, take))
        done += take
        hop += 1
    return pieces


def split_product(data, pair_ref):
    high = data.astype(BF16)
    low = (data - high.astype(F32)).astype(BF16)
    out = jnp.dot(high, pair_ref[0], preferred_element_type=F32)
    out += jnp.dot(low, pair_ref[0], preferred_element_type=F32)
    return out + jnp.dot(high, pair_ref[1], preferred_element_type=F32)


def product_split(pair_ref, data):
    high = data.astype(BF16)
    low = (data - high.astype(F32)).astype(BF16)
    out = jnp.dot(pair_ref[0], high, preferred_element_type=F32)
    out += jnp.dot(pair_ref[0], low, preferred_element_type=F32)
    return out + jnp.dot(pair_ref[1], high, preferred_element_type=F32)


def kernel(levels, nz, ny, count, *refs):
    field = refs[0]
    keeps = refs[1:5]
    coarse = refs[5]
    x_fwd = refs[6:10]
    x_inv = refs[10:14]
    y_fwd = refs[14:18]
    y_inv = refs[18:22]
    out = refs[22]
    whole, mixed_x, mixed_y = refs[23:26]
    exts = (None,) + refs[26:29]
    zbufs = (None,) + refs[29:32]
    coefs = refs[32:36]
    sbufs = refs[36:40]
    ybufs = refs[40:44]
    local_sem, send_sem, recv_sem = refs[44:47]
    gz = lax.axis_index("gz")
    gy = lax.axis_index("gy")

    def device(dz, dy):
        return (lax.rem(gz + (dz + nz) % nz, nz), lax.rem(gy + (dy + ny) % ny, ny))

    load = pltpu.make_async_copy(field, whole, local_sem)
    load.start()
    offsets = sorted(
        {(dz % nz, dy % ny) for dz in range(-5, 6) for dy in range(-2, 3)} - {(0, 0)}
    )
    barrier = pltpu.get_barrier_semaphore()
    for dz, dy in offsets:
        pl.semaphore_signal(barrier, inc=1, device_id=device(dz, dy), device_id_type=MESH)

    used = [0]
    sends = []

    def send(src, dst, dz, dy):
        at = used[0]
        used[0] += 1
        copy = pltpu.make_async_remote_copy(
            src_ref=src,
            dst_ref=dst,
            send_sem=send_sem.at[at],
            recv_sem=recv_sem.at[at],
            device_id=device(dz, dy),
            device_id_type=MESH,
        )
        copy.start()
        sends.append(copy)
        return copy

    def send_rim(lv, source, ext):
        copies = []
        for hz, z_at, z_take in hop_list(lv.z, 10):
            for hy in range(lv.rim_hops + 1):
                if hy and hy % ny == 0 or (hz == 0 and hy == 0):
                    continue
                rows = lv.y if hy == 0 else lv.rim_rows
                z_to = 0 if hz == 0 else lv.z + z_at
                y_to = 0 if hy == 0 else lv.y + (hy - 1) * lv.rim_rows
                copies.append(
                    send(
                        source.at[0:z_take, 0:rows],
                        ext.at[z_to : z_to + z_take, y_to : y_to + rows],
                        -hz,
                        -hy,
                    )
                )
        return copies

    def send_back(lv, coef, first, last, lanes=slice(None)):
        copies = []
        own = lv.back_hops
        for hz, z_at, z_take in hop_list(lv.zc, 5):
            for hy in range(lv.back_hops + 1):
                if hy and hy % ny == 0 or (hz == 0 and hy == 0):
                    continue
                z_from = 5 if hz == 0 else 5 + lv.zc - z_take
                z_to = 5 if hz == 0 else 5 - z_at - z_take
                y_from = own if hy == 0 else lv.blocks - 1
                y_take = lv.blocks - own if hy == 0 else 1
                y_to = own if hy == 0 else own - hy
                copies.append(
                    send(
                        coef.at[first:last, z_from : z_from + z_take, y_from : y_from + y_take, :, lanes],
                        coef.at[first:last, z_to : z_to + z_take, y_to : y_to + y_take, :, lanes],
                        hz,
                        hy,
                    )
                )
        return copies

    first = levels[0]
    half = first.xc
    rim = first.rim_rows
    assert first.rim_hops == 1 and first.z >= 10 and first.back_hops == 1

    load.wait()
    rows = whole[:, 0:rim, :].reshape(first.z * rim, first.x)
    mixed_x[:, 0:rim, :] = split_product(rows, x_fwd[0]).reshape(first.z, rim, first.x)
    pl.semaphore_wait(barrier, len(offsets))
    y_low, y_high = [
        send(
            mixed_x.at[:, 0:rim, lanes],
            mixed_x.at[:, first.y : first.y + rim, lanes],
            0,
            -1,
        )
        for lanes in (slice(0, half), slice(half, first.x))
    ]

    def x_rest(step, carry):
        at = pl.ds(step * 4, 4)
        rest = whole[at, rim : first.y, :].reshape(4 * (first.y - rim), first.x)
        done = split_product(rest, x_fwd[0])
        mixed_x[at, rim : first.y, :] = done.reshape(4, first.y - rim, first.x)
        return carry

    lax.fori_loop(0, first.z // 4, x_rest, 0)

    def y_planes(start, stop, lanes):
        def y_plane(z, carry):
            mixed_y[z, :, lanes] = product_split(y_fwd[0], mixed_x[z, :, lanes])
            return carry

        lax.fori_loop(start, stop, y_plane, 0)

    def z_rim(rows, lanes):
        return send(
            mixed_y.at[0:10, rows, lanes],
            mixed_y.at[first.z : first.z + 10, rows, lanes],
            -1,
            0,
        )

    def z_bands(by, bx):
        lanes = slice(bx * half, (bx + 1) * half)
        at = slice(by * first.yc, (by + 1) * first.yc)

        def z_band(i, carry):
            low = high = None
            for k in range(12):
                part = mixed_y[2 * i + k, at, lanes]
                low = low_taps[k] * part if k == 0 else low + low_taps[k] * part
                high = high_taps[k] * part if k == 0 else high + high_taps[k] * part
            for bz, piece in ((0, low), (1, high)):
                band = 4 * bz + 2 * by + bx
                if band == 0:
                    exts[1][i, 0 : first.yc, :] = piece
                else:
                    piece = piece * keeps[0][band - 1, i].astype(F32)
                    shaped = piece.reshape(first.yc // 8, 8, half)
                    coefs[0][2 * bz + by, 5 + i, 1 : first.blocks, :, lanes] = shaped
            return carry

        lax.fori_loop(0, first.zc, z_band, 0)

    low_lanes, high_lanes = slice(0, half), slice(half, first.x)
    y_low.wait_recv()
    y_planes(0, 10, low_lanes)
    z_first = z_rim(slice(0, first.yc), low_lanes)
    y_planes(10, first.z, low_lanes)
    y_high.wait_recv()
    y_planes(0, 10, high_lanes)
    z_late = [z_rim(slice(first.yc, first.y), low_lanes), z_rim(slice(0, first.y), high_lanes)]
    y_planes(10, first.z, high_lanes)
    z_first.wait_recv()
    z_bands(0, 0)

    early = [None] * LEVELS
    for no, lv in enumerate(levels):
        if no == 0:
            continue
        ext, zbuf, coef, keep = exts[no], zbufs[no], coefs[no], keeps[no]
        copies = send_rim(lv, ext, ext)
        if no == 2:
            early[1] = send_back(levels[1], coefs[1], 1, 4)
            for copy in z_late:
                copy.wait_recv()
            z_bands(0, 1)
            z_bands(1, 0)
            z_bands(1, 1)
            early[0] = send_back(first, coefs[0], 1, 4)
            early[0] += send_back(first, coefs[0], 0, 1, high_lanes)
        if no == 3:
            early[2] = send_back(levels[2], coefs[2], 1, 4)
        for copy in copies:
            copy.wait_recv()
        for hy in range(1, lv.rim_hops + 1):
            if hy % ny == 0:
                y_to = lv.y + (hy - 1) * lv.rim_rows
                ext[:, y_to : y_to + lv.rim_rows, :] = ext[:, 0 : lv.rim_rows, :]
        chunk = 16 if lv.y_ext % 16 == 0 else 8
        steps = lv.y_ext // chunk

        def z_split(step, carry, lv=lv, ext=ext, zbuf=zbuf, chunk=chunk, steps=steps):
            i = step // steps
            row = pl.multiple_of((step % steps) * chunk, chunk)
            low = high = None
            for k in range(12):
                part = ext[2 * i + k, pl.ds(row, chunk), :]
                low = low_taps[k] * part if k == 0 else low + low_taps[k] * part
                high = high_taps[k] * part if k == 0 else high + high_taps[k] * part
            zbuf[i, pl.ds(row, chunk), :] = low
            zbuf[lv.zc + i, pl.ds(row, chunk), :] = high
            return carry

        lax.fori_loop(0, lv.zc * steps, z_split, 0)
        group = min(lv.z, 4)

        def x_split(step, carry, lv=lv, zbuf=zbuf, group=group, no=no):
            at = pl.ds(step * group, group)
            rows = zbuf[at].reshape(group * lv.y_ext, lv.x)
            zbuf[at] = split_product(rows, x_fwd[no]).reshape(group, lv.y_ext, lv.x)
            return carry

        lax.fori_loop(0, lv.z // group, x_split, 0)

        def y_split(i, carry, lv=lv, zbuf=zbuf, coef=coef, keep=keep, no=no):
            for bz in range(2):
                mixed = product_split(y_fwd[no], zbuf[bz * lv.zc + i])
                for by in range(2):
                    part = mixed[by * lv.yc : (by + 1) * lv.yc]
                    for bx in range(2):
                        band = 4 * bz + 2 * by + bx
                        piece = part[:, bx * lv.xc : (bx + 1) * lv.xc]
                        if band:
                            piece = piece * keep[band - 1, i].astype(F32)
                        elif no < LEVELS - 1:
                            exts[no + 1][i, 0 : lv.yc, :] = piece
                            continue
                        else:
                            piece = piece * coarse[i].astype(F32)
                        shaped = piece.reshape(lv.yc // lv.block, lv.block, lv.xc)
                        lanes = slice(bx * lv.xc, (bx + 1) * lv.xc)
                        coef[2 * bz + by, 5 + i, lv.back_hops : lv.blocks, :, lanes] = shaped
            return carry

        lax.fori_loop(0, lv.zc, y_split, 0)

    for no in range(LEVELS - 1, -1, -1):
        lv, coef, sbuf, ybuf = levels[no], coefs[no], sbufs[no], ybufs[no]
        late = send_back(lv, coef, 0, 1, low_lanes if no == 0 else slice(None))
        if no == LEVELS - 1:
            early[no] = send_back(lv, coef, 1, 4)

        def x_merge(b, carry, lv=lv, coef=coef, sbuf=sbuf, no=no):
            if lv.block == 8:
                rows = coef[b].reshape(lv.zc_ext * lv.yc_ext, lv.x)
                sbuf[b] = split_product(rows, x_inv[no]).reshape(lv.zc_ext, lv.yc_ext, lv.x)
            else:
                for z in range(lv.zc_ext):
                    rows = jnp.concatenate([coef[b, z, j] for j in range(lv.blocks)], axis=0)
                    sbuf[b, z] = split_product(rows, x_inv[no])
            return carry

        def y_merge(bz, lv=lv, sbuf=sbuf, ybuf=ybuf, no=no):
            def merge(z, carry):
                pair = jnp.concatenate([sbuf[2 * bz, z], sbuf[2 * bz + 1, z]], axis=0)
                ybuf[bz, z] = product_split(y_inv[no], pair)
                return carry

            lax.fori_loop(0, lv.zc_ext, merge, 0)

        for copies, start, stop in ((early[no], 1, 4), (late, 0, 1)):
            for copy in copies:
                copy.wait_recv()
            for hy in range(1, lv.back_hops + 1):
                if hy % ny == 0:
                    same = coef[start:stop, :, lv.blocks - 1]
                    coef[start:stop, :, lv.back_hops - hy] = same
            lax.fori_loop(start, stop, x_merge, 0)
            y_merge(1 if start else 0)
        chunk = min(lv.y, 16)
        if no:
            chunk = min(chunk, levels[no - 1].block)
        steps = lv.y // chunk

        def z_merge(step, carry, lv=lv, ybuf=ybuf, no=no, chunk=chunk, steps=steps):
            i = step // steps
            at = step % steps
            row = pl.multiple_of(at * chunk, chunk)
            even = odd = None
            for t in range(6):
                low = ybuf[0, i + 5 - t, pl.ds(row, chunk), :]
                high = ybuf[1, i + 5 - t, pl.ds(row, chunk), :]
                even_term = low_taps[2 * t] * low + high_taps[2 * t] * high
                odd_term = low_taps[2 * t + 1] * low + high_taps[2 * t + 1] * high
                even = even_term if t == 0 else even + even_term
                odd = odd_term if t == 0 else odd + odd_term
            for p, value in ((0, even), (1, odd)):
                if no == 0:
                    out[2 * i + p, pl.ds(row, chunk), :] = value
                else:
                    own = levels[no - 1].back_hops
                    coefs[no - 1][0, 5 + 2 * i + p, own + at, :, 0 : lv.x] = value
            return carry

        lax.fori_loop(0, lv.zc * steps, z_merge, 0)
    for copy in sends:
        copy.wait_send()
    assert used[0] <= count


def solution(mesh):
    nz, ny = mesh.shape["gz"], mesh.shape["gy"]

    def on_device(field, k1, k2, k3, k4, coarse):
        z, y, x = field.shape
        levels = [Level(z >> n, y >> n, x >> n) for n in range(LEVELS)]
        count = 128
        x_pairs = [halves(x_matrix(lv.x)) for lv in levels]
        xt_pairs = [halves(x_matrix(lv.x).T) for lv in levels]
        y_pairs = [halves(y_split_matrix(lv.y, lv.y_ext)) for lv in levels]
        yt_pairs = [halves(y_merge_matrix(lv.yc, lv.yc_ext)) for lv in levels]
        mats = [jnp.asarray(m) for m in x_pairs + xt_pairs + y_pairs + yt_pairs]
        vmem = pl.BlockSpec(memory_space=pltpu.VMEM)
        scratch = [pltpu.VMEM((z, y, x), F32)]
        scratch += [pltpu.VMEM((z, levels[0].y_ext, x), F32)]
        scratch += [pltpu.VMEM((levels[0].z_ext, y, x), F32)]
        scratch += [pltpu.VMEM((lv.z_ext, lv.y_ext, lv.x), F32) for lv in levels[1:]]
        scratch += [pltpu.VMEM((lv.z, lv.y_ext, lv.x), F32) for lv in levels[1:]]
        scratch += [pltpu.VMEM((4, lv.zc_ext, lv.blocks, lv.block, lv.x), F32) for lv in levels]
        scratch += [pltpu.VMEM((4, lv.zc_ext, lv.yc_ext, lv.x), F32) for lv in levels]
        scratch += [pltpu.VMEM((2, lv.zc_ext, lv.y, lv.x), F32) for lv in levels]
        scratch += [
            pltpu.SemaphoreType.DMA,
            pltpu.SemaphoreType.DMA((count,)),
            pltpu.SemaphoreType.DMA((count,)),
        ]
        return pl.pallas_call(
            functools.partial(kernel, levels, nz, ny, count),
            out_shape=jax.ShapeDtypeStruct((z, y, x), F32),
            in_specs=[pl.BlockSpec(memory_space=pl.ANY)] + [vmem] * (5 + len(mats)),
            out_specs=vmem,
            scratch_shapes=scratch,
            compiler_params=pltpu.CompilerParams(
                collective_id=0, has_side_effects=True, vmem_limit_bytes=60 * 1024 * 1024
            ),
        )(field, k1, k2, k3, k4, coarse, *mats)

    in_specs = (
        P("gz", "gy", None),
        P(None, "gz", "gy", None),
        P(None, "gz", "gy", None),
        P(None, "gz", "gy", None),
        P(None, "gz", "gy", None),
        P("gz", "gy", None),
    )
    return jax.shard_map(
        on_device, mesh=mesh, in_specs=in_specs, out_specs=P("gz", "gy", None), check_vma=False
    )
```

```python
import functools

import jax
import jax.numpy as jnp
import ml_dtypes
import numpy as np
from jax import lax
from jax.experimental import pallas as pl
from jax.experimental.pallas import tpu as pltpu
from jax.sharding import PartitionSpec as P

low_taps = (
    0.11154074335008017,
    0.4946238903983854,
    0.7511339080215775,
    0.3152503517092432,
    -0.22626469396516913,
    -0.12976686756709563,
    0.09750160558707936,
    0.02752286553001629,
    -0.031582039318031156,
    0.0005538422009938016,
    0.004777257511010651,
    -0.00107730108499558,
)
high_taps = tuple(((-1.0) ** k * low_taps[11 - k] for k in range(12)))
LEVELS = 4
MESH = pl.DeviceIdType.MESH
BF16 = jnp.bfloat16
F32 = jnp.float32


def halves(matrix):
    matrix = matrix.astype(np.float32)
    high = matrix.astype(ml_dtypes.bfloat16)
    low = (matrix - high.astype(np.float32)).astype(ml_dtypes.bfloat16)
    return np.stack([high, low])


def x_matrix(x_len):
    half = x_len // 2
    matrix = np.zeros((x_len, x_len))
    for i in range(half):
        for k in range(12):
            matrix[(2 * i + k) % x_len, i] += low_taps[k]
            matrix[(2 * i + k) % x_len, half + i] += high_taps[k]
    return matrix


def y_split_matrix(y_len, ext_len):
    half = y_len // 2
    matrix = np.zeros((y_len, ext_len))
    for i in range(half):
        for k in range(12):
            matrix[i, 2 * i + k] = low_taps[k]
            matrix[half + i, 2 * i + k] = high_taps[k]
    return matrix


def y_merge_matrix(coarse, ext_len):
    first = ext_len - coarse
    matrix = np.zeros((2 * coarse, 2 * ext_len))
    for j in range(2 * coarse):
        for t in range(6):
            k = 2 * t + j % 2
            c = j // 2 - t + first
            matrix[j, c] = low_taps[k]
            matrix[j, ext_len + c] = high_taps[k]
    return matrix


class Level:
    def __init__(self, z, y, x):
        self.z, self.y, self.x = z, y, x
        self.zc, self.yc, self.xc = z // 2, y // 2, x // 2
        self.rim_rows = min(y, 16)
        self.rim_hops = 16 // self.rim_rows
        self.y_ext = y + 16
        self.z_ext = z + 10
        self.block = min(self.yc, 8)
        self.back_hops = 8 // self.block
        self.blocks = self.yc // self.block + self.back_hops
        self.yc_ext = self.blocks * self.block
        self.zc_ext = self.zc + 5


def hop_list(length, rim):
    pieces = [(0, 0, length)]
    done = 0
    hop = 1
    while done < rim:
        take = min(length, rim - done)
        pieces.append((hop, done, take))
        done += take
        hop += 1
    return pieces


def split_product(data, pair_ref):
    high = data.astype(BF16)
    low = (data - high.astype(F32)).astype(BF16)
    out = jnp.dot(high, pair_ref[0], preferred_element_type=F32)
    out += jnp.dot(low, pair_ref[0], preferred_element_type=F32)
    return out + jnp.dot(high, pair_ref[1], preferred_element_type=F32)


def product_split(pair_ref, data):
    high = data.astype(BF16)
    low = (data - high.astype(F32)).astype(BF16)
    out = jnp.dot(pair_ref[0], high, preferred_element_type=F32)
    out += jnp.dot(pair_ref[0], low, preferred_element_type=F32)
    return out + jnp.dot(pair_ref[1], high, preferred_element_type=F32)


def kernel(levels, nz, ny, count, *refs):
    field = refs[0]
    keeps = refs[1:5]
    coarse = refs[5]
    x_fwd = refs[6:10]
    x_inv = refs[10:14]
    y_fwd = refs[14:18]
    y_inv = refs[18:22]
    out = refs[22]
    whole, mixed_x, mixed_y = refs[23:26]
    exts = (None,) + refs[26:29]
    zbufs = (None,) + refs[29:32]
    coefs = refs[32:36]
    sbufs = refs[36:40]
    ybufs = refs[40:44]
    local_sem, send_sem, recv_sem = refs[44:47]
    gz = lax.axis_index("gz")
    gy = lax.axis_index("gy")

    def device(dz, dy):
        return (lax.rem(gz + (dz + nz) % nz, nz), lax.rem(gy + (dy + ny) % ny, ny))

    load = pltpu.make_async_copy(field, whole, local_sem)
    load.start()
    offsets = sorted(
        {(dz % nz, dy % ny) for dz in range(-5, 6) for dy in range(-2, 3)} - {(0, 0)}
    )
    barrier = pltpu.get_barrier_semaphore()
    for dz, dy in offsets:
        pl.semaphore_signal(barrier, inc=1, device_id=device(dz, dy), device_id_type=MESH)

    used = [0]
    sends = []

    def send(src, dst, dz, dy):
        at = used[0]
        used[0] += 1
        copy = pltpu.make_async_remote_copy(
            src_ref=src,
            dst_ref=dst,
            send_sem=send_sem.at[at],
            recv_sem=recv_sem.at[at],
            device_id=device(dz, dy),
            device_id_type=MESH,
        )
        copy.start()
        sends.append(copy)
        return copy

    def send_rim(lv, source, ext):
        copies = []
        for hz, z_at, z_take in hop_list(lv.z, 10):
            for hy in range(lv.rim_hops + 1):
                if hy and hy % ny == 0 or (hz == 0 and hy == 0):
                    continue
                rows = lv.y if hy == 0 else lv.rim_rows
                z_to = 0 if hz == 0 else lv.z + z_at
                y_to = 0 if hy == 0 else lv.y + (hy - 1) * lv.rim_rows
                copies.append(
                    send(
                        source.at[0:z_take, 0:rows],
                        ext.at[z_to : z_to + z_take, y_to : y_to + rows],
                        -hz,
                        -hy,
                    )
                )
        return copies

    def send_back(lv, coef, first, last, lanes=slice(None)):
        copies = []
        own = lv.back_hops
        for hz, z_at, z_take in hop_list(lv.zc, 5):
            for hy in range(lv.back_hops + 1):
                if hy and hy % ny == 0 or (hz == 0 and hy == 0):
                    continue
                z_from = 5 if hz == 0 else 5 + lv.zc - z_take
                z_to = 5 if hz == 0 else 5 - z_at - z_take
                y_from = own if hy == 0 else lv.blocks - 1
                y_take = lv.blocks - own if hy == 0 else 1
                y_to = own if hy == 0 else own - hy
                copies.append(
                    send(
                        coef.at[first:last, z_from : z_from + z_take, y_from : y_from + y_take, :, lanes],
                        coef.at[first:last, z_to : z_to + z_take, y_to : y_to + y_take, :, lanes],
                        hz,
                        hy,
                    )
                )
        return copies

    first = levels[0]
    half = first.xc
    rim = first.rim_rows
    assert first.rim_hops == 1 and first.z >= 10 and first.back_hops == 1

    load.wait()
    rows = whole[:, 0:rim, :].reshape(first.z * rim, first.x)
    mixed_x[:, 0:rim, :] = split_product(rows, x_fwd[0]).reshape(first.z, rim, first.x)
    pl.semaphore_wait(barrier, len(offsets))
    y_low, y_high = [
        send(
            mixed_x.at[:, 0:rim, lanes],
            mixed_x.at[:, first.y : first.y + rim, lanes],
            0,
            -1,
        )
        for lanes in (slice(0, half), slice(half, first.x))
    ]

    def x_rest(step, carry):
        at = pl.ds(step * 4, 4)
        rest = whole[at, rim : first.y, :].reshape(4 * (first.y - rim), first.x)
        done = split_product(rest, x_fwd[0])
        mixed_x[at, rim : first.y, :] = done.reshape(4, first.y - rim, first.x)
        return carry

    lax.fori_loop(0, first.z // 4, x_rest, 0)

    def y_planes(start, stop, lanes):
        def y_plane(z, carry):
            mixed_y[z, :, lanes] = product_split(y_fwd[0], mixed_x[z, :, lanes])
            return carry

        lax.fori_loop(start, stop, y_plane, 0)

    def z_rim(rows, lanes):
        return send(
            mixed_y.at[0:10, rows, lanes],
            mixed_y.at[first.z : first.z + 10, rows, lanes],
            -1,
            0,
        )

    def z_bands(by, bx):
        lanes = slice(bx * half, (bx + 1) * half)
        at = slice(by * first.yc, (by + 1) * first.yc)

        def z_band(i, carry):
            low = high = None
            for k in range(12):
                part = mixed_y[2 * i + k, at, lanes]
                low = low_taps[k] * part if k == 0 else low + low_taps[k] * part
                high = high_taps[k] * part if k == 0 else high + high_taps[k] * part
            for bz, piece in ((0, low), (1, high)):
                band = 4 * bz + 2 * by + bx
                if band == 0:
                    exts[1][i, 0 : first.yc, :] = piece
                else:
                    piece = piece * keeps[0][band - 1, i].astype(F32)
                    shaped = piece.reshape(first.yc // 8, 8, half)
                    coefs[0][2 * bz + by, 5 + i, 1 : first.blocks, :, lanes] = shaped
            return carry

        lax.fori_loop(0, first.zc, z_band, 0)

    low_lanes, high_lanes = slice(0, half), slice(half, first.x)
    y_low.wait_recv()
    y_planes(0, 10, low_lanes)
    z_first = z_rim(slice(0, first.yc), low_lanes)
    y_planes(10, first.z, low_lanes)
    y_high.wait_recv()
    y_planes(0, 10, high_lanes)
    y_planes(10, first.z, high_lanes)
    z_first.wait_recv()
    z_bands(0, 0)

    early = [None] * LEVELS
    for no, lv in enumerate(levels):
        if no == 0:
            continue
        ext, zbuf, coef, keep = exts[no], zbufs[no], coefs[no], keeps[no]
        copies = send_rim(lv, ext, ext)
        if no == 1:
            z_late = [z_rim(slice(first.yc, first.y), low_lanes)]
        if no == 2:
            z_late.append(z_rim(slice(0, first.y), high_lanes))
        if no == 3:
            early[1] = send_back(levels[1], coefs[1], 1, 4)
            for copy in z_late:
                copy.wait_recv()
            z_bands(0, 1)
            z_bands(1, 0)
            z_bands(1, 1)
        for copy in copies:
            copy.wait_recv()
        for hy in range(1, lv.rim_hops + 1):
            if hy % ny == 0:
                y_to = lv.y + (hy - 1) * lv.rim_rows
                ext[:, y_to : y_to + lv.rim_rows, :] = ext[:, 0 : lv.rim_rows, :]
        chunk = 16 if lv.y_ext % 16 == 0 else 8
        steps = lv.y_ext // chunk

        def z_split(step, carry, lv=lv, ext=ext, zbuf=zbuf, chunk=chunk, steps=steps):
            i = step // steps
            row = pl.multiple_of((step % steps) * chunk, chunk)
            low = high = None
            for k in range(12):
                part = ext[2 * i + k, pl.ds(row, chunk), :]
                low = low_taps[k] * part if k == 0 else low + low_taps[k] * part
                high = high_taps[k] * part if k == 0 else high + high_taps[k] * part
            zbuf[i, pl.ds(row, chunk), :] = low
            zbuf[lv.zc + i, pl.ds(row, chunk), :] = high
            return carry

        lax.fori_loop(0, lv.zc * steps, z_split, 0)
        group = min(lv.z, 4)

        def x_split(step, carry, lv=lv, zbuf=zbuf, group=group, no=no):
            at = pl.ds(step * group, group)
            rows = zbuf[at].reshape(group * lv.y_ext, lv.x)
            zbuf[at] = split_product(rows, x_fwd[no]).reshape(group, lv.y_ext, lv.x)
            return carry

        lax.fori_loop(0, lv.z // group, x_split, 0)

        def y_split(i, carry, lv=lv, zbuf=zbuf, coef=coef, keep=keep, no=no):
            for bz in range(2):
                mixed = product_split(y_fwd[no], zbuf[bz * lv.zc + i])
                for by in range(2):
                    part = mixed[by * lv.yc : (by + 1) * lv.yc]
                    for bx in range(2):
                        band = 4 * bz + 2 * by + bx
                        piece = part[:, bx * lv.xc : (bx + 1) * lv.xc]
                        if band:
                            piece = piece * keep[band - 1, i].astype(F32)
                        elif no < LEVELS - 1:
                            exts[no + 1][i, 0 : lv.yc, :] = piece
                            continue
                        else:
                            piece = piece * coarse[i].astype(F32)
                        shaped = piece.reshape(lv.yc // lv.block, lv.block, lv.xc)
                        lanes = slice(bx * lv.xc, (bx + 1) * lv.xc)
                        coef[2 * bz + by, 5 + i, lv.back_hops : lv.blocks, :, lanes] = shaped
            return carry

        lax.fori_loop(0, lv.zc, y_split, 0)

    for no in range(LEVELS - 1, -1, -1):
        lv, coef, sbuf, ybuf = levels[no], coefs[no], sbufs[no], ybufs[no]
        late = send_back(lv, coef, 0, 1, low_lanes if no == 0 else slice(None))
        if no == LEVELS - 1:
            early[no] = send_back(lv, coef, 1, 4)
            early[2] = send_back(levels[2], coefs[2], 1, 4)
            early[0] = send_back(first, coefs[0], 2, 3)
        if no == 2:
            early[0] += send_back(first, coefs[0], 3, 4)
        if no == 1:
            early[0] += send_back(first, coefs[0], 1, 2)
            early[0] += send_back(first, coefs[0], 0, 1, high_lanes)

        def x_merge(b, carry, lv=lv, coef=coef, sbuf=sbuf, no=no):
            if lv.block == 8:
                rows = coef[b].reshape(lv.zc_ext * lv.yc_ext, lv.x)
                sbuf[b] = split_product(rows, x_inv[no]).reshape(lv.zc_ext, lv.yc_ext, lv.x)
            else:
                for z in range(lv.zc_ext):
                    rows = jnp.concatenate([coef[b, z, j] for j in range(lv.blocks)], axis=0)
                    sbuf[b, z] = split_product(rows, x_inv[no])
            return carry

        def y_merge(bz, lv=lv, sbuf=sbuf, ybuf=ybuf, no=no):
            def merge(z, carry):
                pair = jnp.concatenate([sbuf[2 * bz, z], sbuf[2 * bz + 1, z]], axis=0)
                ybuf[bz, z] = product_split(y_inv[no], pair)
                return carry

            lax.fori_loop(0, lv.zc_ext, merge, 0)

        for copies, start, stop in ((early[no], 1, 4), (late, 0, 1)):
            for copy in copies:
                copy.wait_recv()
            for hy in range(1, lv.back_hops + 1):
                if hy % ny == 0:
                    same = coef[start:stop, :, lv.blocks - 1]
                    coef[start:stop, :, lv.back_hops - hy] = same
            lax.fori_loop(start, stop, x_merge, 0)
            y_merge(1 if start else 0)
        chunk = min(lv.y, 16)
        if no:
            chunk = min(chunk, levels[no - 1].block)
        steps = lv.y // chunk

        def z_merge(step, carry, lv=lv, ybuf=ybuf, no=no, chunk=chunk, steps=steps):
            i = step // steps
            at = step % steps
            row = pl.multiple_of(at * chunk, chunk)
            even = odd = None
            for t in range(6):
                low = ybuf[0, i + 5 - t, pl.ds(row, chunk), :]
                high = ybuf[1, i + 5 - t, pl.ds(row, chunk), :]
                even_term = low_taps[2 * t] * low + high_taps[2 * t] * high
                odd_term = low_taps[2 * t + 1] * low + high_taps[2 * t + 1] * high
                even = even_term if t == 0 else even + even_term
                odd = odd_term if t == 0 else odd + odd_term
            for p, value in ((0, even), (1, odd)):
                if no == 0:
                    out[2 * i + p, pl.ds(row, chunk), :] = value
                else:
                    own = levels[no - 1].back_hops
                    coefs[no - 1][0, 5 + 2 * i + p, own + at, :, 0 : lv.x] = value
            return carry

        lax.fori_loop(0, lv.zc * steps, z_merge, 0)
    for copy in sends:
        copy.wait_send()
    assert used[0] <= count


def solution(mesh):
    nz, ny = mesh.shape["gz"], mesh.shape["gy"]

    def on_device(field, k1, k2, k3, k4, coarse):
        z, y, x = field.shape
        levels = [Level(z >> n, y >> n, x >> n) for n in range(LEVELS)]
        count = 128
        x_pairs = [halves(x_matrix(lv.x)) for lv in levels]
        xt_pairs = [halves(x_matrix(lv.x).T) for lv in levels]
        y_pairs = [halves(y_split_matrix(lv.y, lv.y_ext)) for lv in levels]
        yt_pairs = [halves(y_merge_matrix(lv.yc, lv.yc_ext)) for lv in levels]
        mats = [jnp.asarray(m) for m in x_pairs + xt_pairs + y_pairs + yt_pairs]
        vmem = pl.BlockSpec(memory_space=pltpu.VMEM)
        scratch = [pltpu.VMEM((z, y, x), F32)]
        scratch += [pltpu.VMEM((z, levels[0].y_ext, x), F32)]
        scratch += [pltpu.VMEM((levels[0].z_ext, y, x), F32)]
        scratch += [pltpu.VMEM((lv.z_ext, lv.y_ext, lv.x), F32) for lv in levels[1:]]
        scratch += [pltpu.VMEM((lv.z, lv.y_ext, lv.x), F32) for lv in levels[1:]]
        scratch += [pltpu.VMEM((4, lv.zc_ext, lv.blocks, lv.block, lv.x), F32) for lv in levels]
        scratch += [pltpu.VMEM((4, lv.zc_ext, lv.yc_ext, lv.x), F32) for lv in levels]
        scratch += [pltpu.VMEM((2, lv.zc_ext, lv.y, lv.x), F32) for lv in levels]
        scratch += [
            pltpu.SemaphoreType.DMA,
            pltpu.SemaphoreType.DMA((count,)),
            pltpu.SemaphoreType.DMA((count,)),
        ]
        return pl.pallas_call(
            functools.partial(kernel, levels, nz, ny, count),
            out_shape=jax.ShapeDtypeStruct((z, y, x), F32),
            in_specs=[pl.BlockSpec(memory_space=pl.ANY)] + [vmem] * (5 + len(mats)),
            out_specs=vmem,
            scratch_shapes=scratch,
            compiler_params=pltpu.CompilerParams(
                collective_id=0, has_side_effects=True, vmem_limit_bytes=60 * 1024 * 1024
            ),
        )(field, k1, k2, k3, k4, coarse, *mats)

    in_specs = (
        P("gz", "gy", None),
        P(None, "gz", "gy", None),
        P(None, "gz", "gy", None),
        P(None, "gz", "gy", None),
        P(None, "gz", "gy", None),
        P("gz", "gy", None),
    )
    return jax.shard_map(
        on_device, mesh=mesh, in_specs=in_specs, out_specs=P("gz", "gy", None), check_vma=False
    )
```

```python
import functools

import jax
import jax.numpy as jnp
import ml_dtypes
import numpy as np
from jax import lax
from jax.experimental import pallas as pl
from jax.experimental.pallas import tpu as pltpu
from jax.sharding import PartitionSpec as P

low_taps = (
    0.11154074335008017,
    0.4946238903983854,
    0.7511339080215775,
    0.3152503517092432,
    -0.22626469396516913,
    -0.12976686756709563,
    0.09750160558707936,
    0.02752286553001629,
    -0.031582039318031156,
    0.0005538422009938016,
    0.004777257511010651,
    -0.00107730108499558,
)
high_taps = tuple(((-1.0) ** k * low_taps[11 - k] for k in range(12)))
LEVELS = 4
MESH = pl.DeviceIdType.MESH
BF16 = jnp.bfloat16
F32 = jnp.float32


def halves(matrix):
    matrix = matrix.astype(np.float32)
    high = matrix.astype(ml_dtypes.bfloat16)
    low = (matrix - high.astype(np.float32)).astype(ml_dtypes.bfloat16)
    return np.stack([high, low])


def x_matrix(x_len):
    half = x_len // 2
    matrix = np.zeros((x_len, x_len))
    for i in range(half):
        for k in range(12):
            matrix[(2 * i + k) % x_len, i] += low_taps[k]
            matrix[(2 * i + k) % x_len, half + i] += high_taps[k]
    return matrix


def y_split_matrix(y_len, ext_len):
    half = y_len // 2
    matrix = np.zeros((y_len, ext_len))
    for i in range(half):
        for k in range(12):
            matrix[i, 2 * i + k] = low_taps[k]
            matrix[half + i, 2 * i + k] = high_taps[k]
    return matrix


def y_merge_matrix(coarse, ext_len):
    first = ext_len - coarse
    matrix = np.zeros((2 * coarse, 2 * ext_len))
    for j in range(2 * coarse):
        for t in range(6):
            k = 2 * t + j % 2
            c = j // 2 - t + first
            matrix[j, c] = low_taps[k]
            matrix[j, ext_len + c] = high_taps[k]
    return matrix


class Level:
    def __init__(self, z, y, x):
        self.z, self.y, self.x = z, y, x
        self.zc, self.yc, self.xc = z // 2, y // 2, x // 2
        self.rim_rows = min(y, 16)
        self.rim_hops = 16 // self.rim_rows
        self.y_ext = y + 16
        self.z_ext = z + 10
        self.block = min(self.yc, 8)
        self.back_hops = 8 // self.block
        self.blocks = self.yc // self.block + self.back_hops
        self.yc_ext = self.blocks * self.block
        self.zc_ext = self.zc + 5


def hop_list(length, rim):
    pieces = [(0, 0, length)]
    done = 0
    hop = 1
    while done < rim:
        take = min(length, rim - done)
        pieces.append((hop, done, take))
        done += take
        hop += 1
    return pieces


def split_product(data, pair_ref):
    high = data.astype(BF16)
    low = (data - high.astype(F32)).astype(BF16)
    out = jnp.dot(high, pair_ref[0], preferred_element_type=F32)
    out += jnp.dot(low, pair_ref[0], preferred_element_type=F32)
    return out + jnp.dot(high, pair_ref[1], preferred_element_type=F32)


def product_split(pair_ref, data):
    high = data.astype(BF16)
    low = (data - high.astype(F32)).astype(BF16)
    out = jnp.dot(pair_ref[0], high, preferred_element_type=F32)
    out += jnp.dot(pair_ref[0], low, preferred_element_type=F32)
    return out + jnp.dot(pair_ref[1], high, preferred_element_type=F32)


def kernel(levels, nz, ny, count, *refs):
    field = refs[0]
    keeps = refs[1:5]
    coarse = refs[5]
    x_fwd = refs[6:10]
    x_inv = refs[10:14]
    y_fwd = refs[14:18]
    y_inv = refs[18:22]
    out = refs[22]
    whole, mixed_x, mixed_y = refs[23:26]
    exts = (None,) + refs[26:29]
    zbufs = (None,) + refs[29:32]
    coefs = refs[32:36]
    sbufs = refs[36:40]
    ybufs = refs[40:44]
    local_sem, send_sem, recv_sem, pack_out, pack_in = refs[44:49]
    gz = lax.axis_index("gz")
    gy = lax.axis_index("gy")

    def device(dz, dy):
        return (lax.rem(gz + (dz + nz) % nz, nz), lax.rem(gy + (dy + ny) % ny, ny))

    load = pltpu.make_async_copy(field, whole, local_sem)
    load.start()
    offsets = sorted(
        {(dz % nz, dy % ny) for dz in range(-5, 6) for dy in range(-2, 3)} - {(0, 0)}
    )
    barrier = pltpu.get_barrier_semaphore()
    for dz, dy in offsets:
        pl.semaphore_signal(barrier, inc=1, device_id=device(dz, dy), device_id_type=MESH)

    used = [0]
    sends = []

    def send(src, dst, dz, dy):
        at = used[0]
        used[0] += 1
        copy = pltpu.make_async_remote_copy(
            src_ref=src,
            dst_ref=dst,
            send_sem=send_sem.at[at],
            recv_sem=recv_sem.at[at],
            device_id=device(dz, dy),
            device_id_type=MESH,
        )
        copy.start()
        sends.append(copy)
        return copy

    def send_rim(lv, source, ext):
        copies = []
        for hz, z_at, z_take in hop_list(lv.z, 10):
            for hy in range(lv.rim_hops + 1):
                if hy and hy % ny == 0 or (hz == 0 and hy == 0):
                    continue
                rows = lv.y if hy == 0 else lv.rim_rows
                z_to = 0 if hz == 0 else lv.z + z_at
                y_to = 0 if hy == 0 else lv.y + (hy - 1) * lv.rim_rows
                copies.append(
                    send(
                        source.at[0:z_take, 0:rows],
                        ext.at[z_to : z_to + z_take, y_to : y_to + rows],
                        -hz,
                        -hy,
                    )
                )
        return copies

    def send_back(lv, coef, first, last, lanes=slice(None)):
        copies = []
        own = lv.back_hops
        for hz, z_at, z_take in hop_list(lv.zc, 5):
            for hy in range(lv.back_hops + 1):
                if hy and hy % ny == 0 or (hz == 0 and hy == 0):
                    continue
                z_from = 5 if hz == 0 else 5 + lv.zc - z_take
                z_to = 5 if hz == 0 else 5 - z_at - z_take
                y_from = own if hy == 0 else lv.blocks - 1
                y_take = lv.blocks - own if hy == 0 else 1
                y_to = own if hy == 0 else own - hy
                copies.append(
                    send(
                        coef.at[first:last, z_from : z_from + z_take, y_from : y_from + y_take, :, lanes],
                        coef.at[first:last, z_to : z_to + z_take, y_to : y_to + y_take, :, lanes],
                        hz,
                        hy,
                    )
                )
        return copies

    first = levels[0]
    half = first.xc
    rim = first.rim_rows
    assert first.rim_hops == 1 and first.z >= 10 and first.back_hops == 1

    load.wait()
    rows = whole[:, 0:rim, :].reshape(first.z * rim, first.x)
    mixed_x[:, 0:rim, :] = split_product(rows, x_fwd[0]).reshape(first.z, rim, first.x)
    for g in range(first.z // 4):
        pack_out[g] = jnp.concatenate(
            [mixed_x[4 * g + j, 8:16, :][0:2] for j in range(4)], axis=0
        )
    pl.semaphore_wait(barrier, len(offsets))
    y_low, y_high = [
        (
            send(
                mixed_x.at[:, 0:8, lanes],
                mixed_x.at[:, first.y : first.y + 8, lanes],
                0,
                -1,
            ),
            send(pack_out.at[:, :, lanes], pack_in.at[:, :, lanes], 0, -1),
        )
        for lanes in (slice(0, half), slice(half, first.x))
    ]

    def take_y(copies, lanes):
        for copy in copies:
            copy.wait_recv()
        empty = jnp.zeros((6, half), F32)
        for z in range(first.z):
            at = 2 * (z % 4)
            piece = pack_in[z // 4, :, lanes][at : at + 2]
            mixed_x[z, first.y + 8 : first.y + 16, lanes] = jnp.concatenate([piece, empty], axis=0)

    def x_rest(step, carry):
        at = pl.ds(step * 4, 4)
        rest = whole[at, rim : first.y, :].reshape(4 * (first.y - rim), first.x)
        done = split_product(rest, x_fwd[0])
        mixed_x[at, rim : first.y, :] = done.reshape(4, first.y - rim, first.x)
        return carry

    lax.fori_loop(0, first.z // 4, x_rest, 0)

    def y_planes(start, stop, lanes):
        def y_plane(z, carry):
            mixed_y[z, :, lanes] = product_split(y_fwd[0], mixed_x[z, :, lanes])
            return carry

        lax.fori_loop(start, stop, y_plane, 0)

    def z_rim(rows, lanes):
        return send(
            mixed_y.at[0:10, rows, lanes],
            mixed_y.at[first.z : first.z + 10, rows, lanes],
            -1,
            0,
        )

    def z_bands(by, bx):
        lanes = slice(bx * half, (bx + 1) * half)
        at = slice(by * first.yc, (by + 1) * first.yc)

        def z_band(i, carry):
            low = high = None
            for k in range(12):
                part = mixed_y[2 * i + k, at, lanes]
                low = low_taps[k] * part if k == 0 else low + low_taps[k] * part
                high = high_taps[k] * part if k == 0 else high + high_taps[k] * part
            for bz, piece in ((0, low), (1, high)):
                band = 4 * bz + 2 * by + bx
                if band == 0:
                    exts[1][i, 0 : first.yc, :] = piece
                else:
                    piece = piece * keeps[0][band - 1, i].astype(F32)
                    shaped = piece.reshape(first.yc // 8, 8, half)
                    coefs[0][2 * bz + by, 5 + i, 1 : first.blocks, :, lanes] = shaped
            return carry

        lax.fori_loop(0, first.zc, z_band, 0)

    low_lanes, high_lanes = slice(0, half), slice(half, first.x)
    take_y(y_low, low_lanes)
    y_planes(0, 10, low_lanes)
    z_first = z_rim(slice(0, first.yc), low_lanes)
    y_planes(10, first.z, low_lanes)
    z_first.wait_recv()
    z_bands(0, 0)

    early = [None] * LEVELS
    for no, lv in enumerate(levels):
        if no == 0:
            continue
        ext, zbuf, coef, keep = exts[no], zbufs[no], coefs[no], keeps[no]
        copies = send_rim(lv, ext, ext)
        if no == 1:
            z_late = [z_rim(slice(first.yc, first.y), low_lanes)]
            take_y(y_high, high_lanes)
            y_planes(0, first.z, high_lanes)
        if no == 2:
            z_late.append(z_rim(slice(0, first.y), high_lanes))
        if no == 3:
            early[1] = send_back(levels[1], coefs[1], 1, 4)
            for copy in z_late:
                copy.wait_recv()
            z_bands(0, 1)
            z_bands(1, 0)
            z_bands(1, 1)
        for copy in copies:
            copy.wait_recv()
        for hy in range(1, lv.rim_hops + 1):
            if hy % ny == 0:
                y_to = lv.y + (hy - 1) * lv.rim_rows
                ext[:, y_to : y_to + lv.rim_rows, :] = ext[:, 0 : lv.rim_rows, :]
        chunk = 16 if lv.y_ext % 16 == 0 else 8
        steps = lv.y_ext // chunk

        def z_split(step, carry, lv=lv, ext=ext, zbuf=zbuf, chunk=chunk, steps=steps):
            i = step // steps
            row = pl.multiple_of((step % steps) * chunk, chunk)
            low = high = None
            for k in range(12):
                part = ext[2 * i + k, pl.ds(row, chunk), :]
                low = low_taps[k] * part if k == 0 else low + low_taps[k] * part
                high = high_taps[k] * part if k == 0 else high + high_taps[k] * part
            zbuf[i, pl.ds(row, chunk), :] = low
            zbuf[lv.zc + i, pl.ds(row, chunk), :] = high
            return carry

        lax.fori_loop(0, lv.zc * steps, z_split, 0)
        group = min(lv.z, 4)

        def x_split(step, carry, lv=lv, zbuf=zbuf, group=group, no=no):
            at = pl.ds(step * group, group)
            rows = zbuf[at].reshape(group * lv.y_ext, lv.x)
            zbuf[at] = split_product(rows, x_fwd[no]).reshape(group, lv.y_ext, lv.x)
            return carry

        lax.fori_loop(0, lv.z // group, x_split, 0)

        def y_split(i, carry, lv=lv, zbuf=zbuf, coef=coef, keep=keep, no=no):
            for bz in range(2):
                mixed = product_split(y_fwd[no], zbuf[bz * lv.zc + i])
                for by in range(2):
                    part = mixed[by * lv.yc : (by + 1) * lv.yc]
                    for bx in range(2):
                        band = 4 * bz + 2 * by + bx
                        piece = part[:, bx * lv.xc : (bx + 1) * lv.xc]
                        if band:
                            piece = piece * keep[band - 1, i].astype(F32)
                        elif no < LEVELS - 1:
                            exts[no + 1][i, 0 : lv.yc, :] = piece
                            continue
                        else:
                            piece = piece * coarse[i].astype(F32)
                        shaped = piece.reshape(lv.yc // lv.block, lv.block, lv.xc)
                        lanes = slice(bx * lv.xc, (bx + 1) * lv.xc)
                        coef[2 * bz + by, 5 + i, lv.back_hops : lv.blocks, :, lanes] = shaped
            return carry

        lax.fori_loop(0, lv.zc, y_split, 0)

    for no in range(LEVELS - 1, -1, -1):
        lv, coef, sbuf, ybuf = levels[no], coefs[no], sbufs[no], ybufs[no]
        late = send_back(lv, coef, 0, 1, low_lanes if no == 0 else slice(None))
        if no == LEVELS - 1:
            early[no] = send_back(lv, coef, 1, 4)
            early[2] = send_back(levels[2], coefs[2], 1, 4)
            early[0] = send_back(first, coefs[0], 2, 3)
        if no == 2:
            early[0] += send_back(first, coefs[0], 3, 4)
        if no == 1:
            early[0] += send_back(first, coefs[0], 1, 2)
            early[0] += send_back(first, coefs[0], 0, 1, high_lanes)

        def x_merge(b, carry, lv=lv, coef=coef, sbuf=sbuf, no=no):
            if lv.block == 8:
                rows = coef[b].reshape(lv.zc_ext * lv.yc_ext, lv.x)
                sbuf[b] = split_product(rows, x_inv[no]).reshape(lv.zc_ext, lv.yc_ext, lv.x)
            else:
                for z in range(lv.zc_ext):
                    rows = jnp.concatenate([coef[b, z, j] for j in range(lv.blocks)], axis=0)
                    sbuf[b, z] = split_product(rows, x_inv[no])
            return carry

        def y_merge(bz, lv=lv, sbuf=sbuf, ybuf=ybuf, no=no):
            def merge(z, carry):
                pair = jnp.concatenate([sbuf[2 * bz, z], sbuf[2 * bz + 1, z]], axis=0)
                ybuf[bz, z] = product_split(y_inv[no], pair)
                return carry

            lax.fori_loop(0, lv.zc_ext, merge, 0)

        for copies, start, stop in ((early[no], 1, 4), (late, 0, 1)):
            for copy in copies:
                copy.wait_recv()
            for hy in range(1, lv.back_hops + 1):
                if hy % ny == 0:
                    same = coef[start:stop, :, lv.blocks - 1]
                    coef[start:stop, :, lv.back_hops - hy] = same
            lax.fori_loop(start, stop, x_merge, 0)
            y_merge(1 if start else 0)
        chunk = min(lv.y, 16)
        if no:
            chunk = min(chunk, levels[no - 1].block)
        steps = lv.y // chunk

        def z_merge(step, carry, lv=lv, ybuf=ybuf, no=no, chunk=chunk, steps=steps):
            i = step // steps
            at = step % steps
            row = pl.multiple_of(at * chunk, chunk)
            even = odd = None
            for t in range(6):
                low = ybuf[0, i + 5 - t, pl.ds(row, chunk), :]
                high = ybuf[1, i + 5 - t, pl.ds(row, chunk), :]
                even_term = low_taps[2 * t] * low + high_taps[2 * t] * high
                odd_term = low_taps[2 * t + 1] * low + high_taps[2 * t + 1] * high
                even = even_term if t == 0 else even + even_term
                odd = odd_term if t == 0 else odd + odd_term
            for p, value in ((0, even), (1, odd)):
                if no == 0:
                    out[2 * i + p, pl.ds(row, chunk), :] = value
                else:
                    own = levels[no - 1].back_hops
                    coefs[no - 1][0, 5 + 2 * i + p, own + at, :, 0 : lv.x] = value
            return carry

        lax.fori_loop(0, lv.zc * steps, z_merge, 0)
    for copy in sends:
        copy.wait_send()
    assert used[0] <= count


def solution(mesh):
    nz, ny = mesh.shape["gz"], mesh.shape["gy"]

    def on_device(field, k1, k2, k3, k4, coarse):
        z, y, x = field.shape
        levels = [Level(z >> n, y >> n, x >> n) for n in range(LEVELS)]
        count = 128
        x_pairs = [halves(x_matrix(lv.x)) for lv in levels]
        xt_pairs = [halves(x_matrix(lv.x).T) for lv in levels]
        y_pairs = [halves(y_split_matrix(lv.y, lv.y_ext)) for lv in levels]
        yt_pairs = [halves(y_merge_matrix(lv.yc, lv.yc_ext)) for lv in levels]
        mats = [jnp.asarray(m) for m in x_pairs + xt_pairs + y_pairs + yt_pairs]
        vmem = pl.BlockSpec(memory_space=pltpu.VMEM)
        scratch = [pltpu.VMEM((z, y, x), F32)]
        scratch += [pltpu.VMEM((z, levels[0].y_ext, x), F32)]
        scratch += [pltpu.VMEM((levels[0].z_ext, y, x), F32)]
        scratch += [pltpu.VMEM((lv.z_ext, lv.y_ext, lv.x), F32) for lv in levels[1:]]
        scratch += [pltpu.VMEM((lv.z, lv.y_ext, lv.x), F32) for lv in levels[1:]]
        scratch += [pltpu.VMEM((4, lv.zc_ext, lv.blocks, lv.block, lv.x), F32) for lv in levels]
        scratch += [pltpu.VMEM((4, lv.zc_ext, lv.yc_ext, lv.x), F32) for lv in levels]
        scratch += [pltpu.VMEM((2, lv.zc_ext, lv.y, lv.x), F32) for lv in levels]
        scratch += [
            pltpu.SemaphoreType.DMA,
            pltpu.SemaphoreType.DMA((count,)),
            pltpu.SemaphoreType.DMA((count,)),
            pltpu.VMEM((z // 4, 8, x), F32),
            pltpu.VMEM((z // 4, 8, x), F32),
        ]
        return pl.pallas_call(
            functools.partial(kernel, levels, nz, ny, count),
            out_shape=jax.ShapeDtypeStruct((z, y, x), F32),
            in_specs=[pl.BlockSpec(memory_space=pl.ANY)] + [vmem] * (5 + len(mats)),
            out_specs=vmem,
            scratch_shapes=scratch,
            compiler_params=pltpu.CompilerParams(
                collective_id=0, has_side_effects=True, vmem_limit_bytes=60 * 1024 * 1024
            ),
        )(field, k1, k2, k3, k4, coarse, *mats)

    in_specs = (
        P("gz", "gy", None),
        P(None, "gz", "gy", None),
        P(None, "gz", "gy", None),
        P(None, "gz", "gy", None),
        P(None, "gz", "gy", None),
        P("gz", "gy", None),
    )
    return jax.shard_map(
        on_device, mesh=mesh, in_specs=in_specs, out_specs=P("gz", "gy", None), check_vma=False
    )
```
